32 devices in a mesh: grp: 2 (over y), seq: 8 (over z, x), head: 2 (over core).
Axes of the slice: x: 2, y: 2, z: 4, core: 2. Of those that a mesh axis runs over, the one named last changes fastest.
Arguments:
- queries: bfloat16 [8192, 4096], P(('grp', 'seq'), 'head'), parts along dimension 0, may hold values from -64 to 64
- keys: bfloat16 [8192, 512], P(('grp', 'seq'), 'head'), parts along dimension 0, may hold values from -6 to 6
- values: bfloat16 [8192, 512], P(('grp', 'seq'), 'head'), parts along dimension 0, may hold values from -6 to 6
- levels: int32 [8192], P(('grp', 'seq')), parts along dimension 0, may hold values from 0 to 3
- members: int32 [16, 4], P(('grp', 'seq')), parts along dimension 0, may hold values from -1 to 31, as said below
Outputs:
- attended: bfloat16 [8192, 4096], P(('grp', 'seq'), 'head'), parts along dimension 0
The draws below stay inside these ranges and needn't reach their ends.
There are 2 independent parts, one for each index of `grp`. The reference program is written for one: setup_inputs(seed, part) draws one part's arguments, and reference() takes and returns one part's arrays. A program takes and returns all parts, laid end to end along the dimension named above; each array names one. Nothing has to cross between parts.
Inputs may be any that keep to these rules, and one draw needn't show every extreme that they name: `members`: slot j of row d is -1 or one of the 4 blocks of group d + o_j; a slot whose group lies outside 0 to 7 is -1; some group lists a block in every slot.
All inputs are finite; a program needn't handle non-finite values.
Results may differ from the reference program's by a relative error of at most 0.005.
Values may be sent and summed in bfloat16 or wider, within the bound.
No kernel may reach another device: no remote copies, remote signals or barrier semaphores. Data moves between devices by JAX's collectives and lax.ppermute only.
A program may use at most 128 MiB of HBM per device.

```python
import jax
import jax.numpy as jnp
from jax import lax

HD = 128
QHEADS = 32
KVHEADS = 4
BLOCK = 128
TOK_DEV = 512
RADIUS = 2
LEVELS = 4
BLK_DEV = 4
TOKENS = 4096
NBLK = 32
N_SEQ = 8


def draw_pair(key):
    base_key = jax.random.fold_in(key, 7301)
    query_key = jax.random.fold_in(base_key, 1)
    key_key = jax.random.fold_in(base_key, 2)
    query_vals = jnp.clip(jax.random.normal(query_key, (TOKENS, QHEADS * HD), jnp.float32), -5.0, 5.0)
    key_vals = jnp.clip(jax.random.normal(key_key, (TOKENS, KVHEADS * HD), jnp.float32), -5.0, 5.0)
    return (query_vals, key_vals)


def draw_queries(key, part):
    return draw_pair(key)[0].astype(jnp.bfloat16)


def draw_keys(key, part):
    return draw_pair(key)[1].astype(jnp.bfloat16)


def draw_members(key, part):
    seq_count = TOKENS // TOK_DEV
    pick_key = jax.random.fold_in(key, 501)
    keep_key = jax.random.fold_in(key, 502)
    groups = jnp.arange(seq_count, dtype=jnp.int32)[:, None]
    offsets = jnp.concatenate([jnp.arange(-RADIUS, 0, dtype=jnp.int32), jnp.arange(1, RADIUS + 1, dtype=jnp.int32)])[None, :]
    owner = groups + offsets
    inside = jnp.logical_and(owner >= 0, owner < seq_count)
    picked = jax.random.randint(pick_key, (seq_count, 2 * RADIUS), 0, BLK_DEV, dtype=jnp.int32)
    kept = jax.random.randint(keep_key, (seq_count, 2 * RADIUS), 0, 4, dtype=jnp.int32) > 0
    full_row = groups == seq_count // 2
    last_slot = jnp.logical_and(groups == seq_count - 2, offsets == 1)
    picked = jnp.where(last_slot, BLK_DEV - 1, picked)
    chosen = jnp.logical_and(inside, jnp.logical_or(jnp.logical_or(kept, full_row), last_slot))
    return jnp.where(chosen, owner * BLK_DEV + picked, -1).astype(jnp.int32)


def plant(entries, own_key, smallest, largest):
    extent = entries.shape
    spot = [jax.random.randint(jax.random.fold_in(own_key, axis), (), 0, extent[axis]) for axis in range(len(extent))]
    entries = entries.at[tuple(spot)].set(smallest)
    longest = extent.index(max(extent))
    spot[longest] = (spot[longest] + 1) % extent[longest]
    return entries.at[tuple(spot)].set(largest)


def steps_of(own_key, shape, pieces, smallest, top_value):
    def one(position, shards_of):
        heights = jax.random.uniform(jax.random.fold_in(jax.random.fold_in(own_key, 6), position), (shards_of,), jnp.float32, smallest / len(pieces), top_value / len(pieces))
        return jnp.repeat(jnp.exp(heights), shape[position] // shards_of).reshape((-1,) + (1,) * (len(shape) - position - 1))

    loudness = one(*pieces[0])
    for cut in pieces[1:]:
        loudness = loudness * one(*cut)
    return loudness


def centred(key, shape, scale, limit, cuts=(), kind=jnp.bfloat16):
    gain = steps_of(key, shape, cuts, -0.22, 0.18) if cuts else 1.0
    drawn = jax.random.normal(key, shape, jnp.float32) * scale * gain
    return jnp.minimum(jnp.maximum(drawn, -limit), limit).astype(kind)


def setup_inputs(seed: int = 0, part: int = 0) -> dict:
    seeds = jax.random.split(jax.random.key(seed), 6)
    part_splits = jax.random.split(jax.random.fold_in(seeds[5], part), 6)
    return {
        "queries": draw_queries(jax.random.fold_in(jax.random.fold_in(seeds[5], part), 71), part),
        "keys": draw_keys(jax.random.fold_in(jax.random.fold_in(seeds[5], part), 71), part),
        "values": centred(part_splits[2], (TOKENS, KVHEADS * HD), 1.0, 6.0, ((0, 8), (1, 2))),
        "levels": plant(jax.random.randint(part_splits[3], (TOKENS,), 0, LEVELS), jax.random.fold_in(part_splits[3], 1), 0, LEVELS - 1).astype(jnp.int32),
        "members": draw_members(jax.random.fold_in(jax.random.fold_in(seeds[5], part), 71), part),
    }


def reference(queries, keys, values, levels, members):
    group_size = QHEADS // KVHEADS
    scaling = HD ** -0.5
    key_blocks = keys.reshape(NBLK, BLOCK, KVHEADS, HD)
    value_blocks = values.reshape(NBLK, BLOCK, KVHEADS, HD)
    level_blocks = levels.reshape(NBLK, BLOCK)

    def one_group(index):
        start = index * TOK_DEV
        query_heads = lax.dynamic_slice_in_dim(queries, start, TOK_DEV, 0).reshape(TOK_DEV, KVHEADS, group_size, HD).astype(jnp.float32)
        own_keys = lax.dynamic_slice_in_dim(keys, start, TOK_DEV, 0).reshape(TOK_DEV, KVHEADS, HD)
        own_values = lax.dynamic_slice_in_dim(values, start, TOK_DEV, 0).reshape(TOK_DEV, KVHEADS, HD)
        own_levels = lax.dynamic_slice_in_dim(levels, start, TOK_DEV, 0)
        listed = members[index]
        safe = jnp.maximum(listed, 0).astype(jnp.int32)
        far_keys = key_blocks[safe].reshape(2 * RADIUS * BLOCK, KVHEADS, HD)
        far_values = value_blocks[safe].reshape(2 * RADIUS * BLOCK, KVHEADS, HD)
        far_levels = level_blocks[safe].reshape(2 * RADIUS * BLOCK)
        far_active = jnp.repeat(listed >= 0, BLOCK)
        all_keys = jnp.concatenate([own_keys, far_keys], axis=0).astype(jnp.float32)
        all_values = jnp.concatenate([own_values, far_values], axis=0).astype(jnp.float32)
        all_levels = jnp.concatenate([own_levels, far_levels], axis=0)
        all_active = jnp.concatenate([jnp.ones((TOK_DEV,), dtype=bool), far_active], axis=0)
        scores = jnp.einsum("tkgd,skd->tkgs", query_heads, all_keys) * scaling
        visible = jnp.logical_and(all_active[None, :], all_levels[None, :] <= own_levels[:, None])
        scores = jnp.where(visible[:, None, None, :], scores, -1e30)
        highest = jnp.max(scores, axis=-1, keepdims=True)
        weights = jnp.exp(scores - highest)
        total = jnp.sum(weights, axis=-1)
        rounded = lax.optimization_barrier(weights.astype(jnp.bfloat16)).astype(jnp.float32)
        mixed = jnp.einsum("tkgs,skd->tkgd", rounded, all_values) / total[..., None]
        return mixed.reshape(TOK_DEV, QHEADS * HD).astype(jnp.bfloat16)

    result = lax.map(one_group, jnp.arange(N_SEQ, dtype=jnp.int32))
    return result.reshape(TOKENS, QHEADS * HD)
```

```python
import functools

import jax
import jax.numpy as jnp
from jax import lax
from jax.experimental import pallas as pl
from jax.experimental.pallas import tpu as pltpu
from jax.sharding import PartitionSpec as P

HD = 128
BLOCK = 128
RADIUS = 2
GROUP = 8
ROWS = 128
PAD = 16
SCALE = HD ** (-0.5) * 1.4426950408889634
HIDDEN = -1e30
NT = (((1,), (1,)), ((), ()))
NN = (((1,), (0,)), ((), ()))


def column_of(row):
    return jnp.broadcast_to(row, (HD, row.shape[1])).T


def bias_of(query_level, key_level):
    wide = jnp.concatenate([query_level] * (key_level.shape[1] // HD), axis=1)
    return jnp.where(key_level <= wide, 0.0, HIDDEN)


def own_kernel(kv_heads, q_ref, k_ref, v_ref, level_ref, o_ref, lse_ref, bias_ref, vx_ref):
    tok = q_ref.shape[0]
    level = level_ref[...].astype(jnp.float32)
    bias_ref[...] = bias_of(column_of(level), level)
    lane = lax.broadcasted_iota(jnp.int32, (ROWS, HD), 1)
    vx_ref[:, HD:] = jnp.ones((tok, HD), jnp.bfloat16)
    lse_ref[...] = jnp.zeros_like(lse_ref)

    def step(g, carry):
        base = pl.multiple_of(g * (GROUP * HD), GROUP * HD)
        cols = pl.ds(pl.multiple_of(g * HD, HD), HD)
        vx_ref[:, :HD] = v_ref[:, cols]
        for r in range(0, tok, ROWS):
            rows = pl.ds(r, ROWS)
            lse = lse_ref[rows, :]
            for h in range(GROUP):
                head = pl.ds(base + h * HD, HD)
                s = lax.dot_general(q_ref[rows, head], k_ref[:, cols], NT, preferred_element_type=jnp.float32)
                s = s * SCALE + bias_ref[rows, :]
                top = jnp.max(s, axis=1, keepdims=True)
                p = jnp.exp2(s - top).astype(jnp.bfloat16)
                o = lax.dot_general(p, vx_ref[...], NN, preferred_element_type=jnp.float32)
                total = o[:, HD:]
                o_ref[rows, head] = o[:, :HD] / total
                lse = jnp.where(lane == g * GROUP + h, top + jnp.log2(total), lse)
            lse_ref[rows, :] = lse
        return carry

    lax.fori_loop(0, kv_heads, step, 0)


def far_kernel(
    kv_heads, pick_ref, q_ref, level_ref, o_ref, lse_ref, lo_ref, near_ref, diag_ref, hi_ref, out_ref,
    bias_ref, kx_ref, vx_ref, kl_ref,
):
    tok = q_ref.shape[0]
    g = pl.program_id(0)
    far = kx_ref.shape[0]

    @pl.when(g == 0)
    def _():
        for slot, (ref, index) in enumerate(((lo_ref, 0), (near_ref, 1), (diag_ref, 2), (hi_ref, 3))):
            if ref is diag_ref:
                level = ref[BLOCK : BLOCK + 1, :BLOCK]
            else:
                first = pl.multiple_of(pick_ref[index] * BLOCK, BLOCK)
                level = ref[tok : tok + 1, pl.ds(first, BLOCK)]
            level = level.astype(jnp.float32)
            kl_ref[0:1, slot * BLOCK : (slot + 1) * BLOCK] = jnp.where(pick_ref[4 + index] > 0, level, 1e9)
        query_level = column_of(level_ref[...].astype(jnp.float32))
        bias_ref[...] = bias_of(query_level, kl_ref[0:1, :])
        vx_ref[:, HD:] = jnp.ones((far, HD), jnp.bfloat16)

    cols = pl.ds(pl.multiple_of(g * HD, HD), HD)
    vcols = pl.ds(pl.multiple_of((g + kv_heads) * HD, HD), HD)
    for slot, (ref, index) in enumerate(((lo_ref, 0), (near_ref, 1), (diag_ref, 2), (hi_ref, 3))):
        if ref is diag_ref:
            first = pl.ds(0, BLOCK)
        else:
            first = pl.ds(pl.multiple_of(pick_ref[index] * BLOCK, BLOCK), BLOCK)
        kx_ref[slot * BLOCK : (slot + 1) * BLOCK, :] = ref[first, cols]
        vx_ref[slot * BLOCK : (slot + 1) * BLOCK, :HD] = ref[first, vcols]
    lane = lax.broadcasted_iota(jnp.int32, (ROWS, HD), 1)
    for r in range(0, tok, ROWS):
        rows = pl.ds(r, ROWS)
        lse_all = lse_ref[rows, :]
        for h in range(GROUP):
            head = pl.ds(pl.multiple_of(g * (GROUP * HD), GROUP * HD) + h * HD, HD)
            own = jnp.max(jnp.where(lane == g * GROUP + h, lse_all, HIDDEN), axis=1, keepdims=True)
            s = lax.dot_general(q_ref[rows, head], kx_ref[...], NT, preferred_element_type=jnp.float32)
            s = s * SCALE + bias_ref[rows, :]
            top = jnp.maximum(jnp.max(s, axis=1, keepdims=True), own)
            p = jnp.exp2(s - top).astype(jnp.bfloat16)
            o = lax.dot_general(p, vx_ref[...], NN, preferred_element_type=jnp.float32)
            share = jnp.exp2(own - top)
            mixed = (o[:, :HD] + share * o_ref[rows, head]) / (o[:, HD:] + share)
            out_ref[rows, h * HD : (h + 1) * HD] = mixed.astype(jnp.bfloat16)


def pairs_of(size, kind):
    if kind == "near":
        edges = [(i, i + 1) for i in range(0, size - 1, 2)]
        return [p for a, b in edges for p in ((a, b), (b, a))]
    if kind == "diag":
        edges = [(i, i + 1) for i in range(1, size - 1, 2)]
        return [p for a, b in edges for p in ((a, b), (b, a))]
    return [(i, i + kind) for i in range(size) if 0 <= i + kind < size]


def local(queries, keys, values, levels, members):
    tok = queries.shape[0]
    kv_heads = keys.shape[1] // HD
    heads = queries.shape[1] // HD
    size = lax.axis_size("seq")
    position = lax.axis_index("seq")
    blocks = tok // BLOCK
    odd = lax.rem(position, 2)
    send = lambda array, kind: lax.ppermute(array, "seq", pairs_of(size, kind))

    width = 2 * keys.shape[1]
    level_row = jnp.pad(levels.astype(jnp.bfloat16)[None, :], ((0, PAD - 1), (0, width - tok)))
    load = jnp.concatenate([jnp.concatenate([keys, values], axis=1), level_row], axis=0)
    from_hi = send(load, -2)
    from_lo = send(load, 2)
    from_near = send(load, "near")

    asked = send(members, "diag")[0]
    asked = jnp.where(odd == 1, asked[1], asked[2])
    first = jnp.clip(asked - position * blocks, 0, blocks - 1) * BLOCK
    piece = lax.dynamic_slice_in_dim(load, first, BLOCK, 0)
    piece_level = jnp.pad(
        lax.dynamic_slice_in_dim(level_row, first, BLOCK, 1), ((0, 0), (0, width - BLOCK))
    )
    from_diag = send(jnp.concatenate([piece, piece_level], axis=0), "diag")

    level_line = levels[None, :]
    vmem = pl.BlockSpec(memory_space=pltpu.VMEM)
    part, lse = pl.pallas_call(
        functools.partial(own_kernel, kv_heads),
        in_specs=[vmem] * 4,
        out_specs=[vmem] * 2,
        out_shape=[
            jax.ShapeDtypeStruct((tok, heads * HD), jnp.float32),
            jax.ShapeDtypeStruct((tok, HD), jnp.float32),
        ],
        scratch_shapes=[pltpu.VMEM((tok, tok), jnp.float32), pltpu.VMEM((tok, 2 * HD), jnp.bfloat16)],
        compiler_params=pltpu.CompilerParams(vmem_limit_bytes=24 << 20),
        cost_estimate=pl.CostEstimate(
            flops=4 * tok * tok * heads * HD, transcendentals=tok * tok * heads, bytes_accessed=8 << 20
        ),
    )(queries, keys, values, level_line)

    row = members[0]
    near_slot = jnp.where(odd == 1, 1, 2)
    order = jnp.stack([row[0], jnp.where(odd == 1, row[1], row[2]), jnp.where(odd == 1, row[2], row[1]), row[3]])
    owner = position + jnp.stack([-2, 1 - 2 * odd, 2 * odd - 1, 2])
    pick = jnp.concatenate(
        [jnp.clip(order - owner * blocks, 0, blocks - 1), (order >= 0).astype(jnp.int32)]
    ).astype(jnp.int32)
    far = 2 * RADIUS * BLOCK
    full = lambda array: pl.BlockSpec(array.shape, lambda g, pick: (0, 0))
    return pl.pallas_call(
        functools.partial(far_kernel, kv_heads),
        grid_spec=pltpu.PrefetchScalarGridSpec(
            num_scalar_prefetch=1,
            grid=(kv_heads,),
            in_specs=[vmem] * 8,
            out_specs=pl.BlockSpec((tok, GROUP * HD), lambda g, pick: (0, g)),
            scratch_shapes=[
                pltpu.VMEM((tok, far), jnp.float32),
                pltpu.VMEM((far, HD), jnp.bfloat16),
                pltpu.VMEM((far, 2 * HD), jnp.bfloat16),
                pltpu.VMEM((8, far), jnp.float32),
            ],
        ),
        out_shape=jax.ShapeDtypeStruct((tok, heads * HD), jnp.bfloat16),
        compiler_params=pltpu.CompilerParams(vmem_limit_bytes=24 << 20),
        cost_estimate=pl.CostEstimate(
            flops=4 * tok * far * heads * HD, transcendentals=tok * far * heads, bytes_accessed=8 << 20
        ),
    )(pick, queries, level_line, part, lse, from_lo, from_near, from_diag, from_hi)


def solution(mesh):
    placed = (
        P(("grp", "seq"), "head"),
        P(("grp", "seq"), "head"),
        P(("grp", "seq"), "head"),
        P(("grp", "seq")),
        P(("grp", "seq"), None),
    )
    return jax.shard_map(
        local, mesh=mesh, in_specs=placed, out_specs=P(("grp", "seq"), "head"), check_vma=False
    )
```

```python
import functools

import jax
import jax.numpy as jnp
from jax import lax
from jax.experimental import pallas as pl
from jax.experimental.pallas import tpu as pltpu
from jax.sharding import PartitionSpec as P

HD = 128
BLOCK = 128
RADIUS = 2
GROUP = 8
ROWS = 128
PAD = 16
SCALE = HD ** (-0.5) * 1.4426950408889634
HIDDEN = -1e30
NT = (((1,), (1,)), ((), ()))
NN = (((1,), (0,)), ((), ()))
VMEM = pl.BlockSpec(memory_space=pltpu.VMEM)
SMEM = pl.BlockSpec(memory_space=pltpu.SMEM)
HBM = pl.BlockSpec(memory_space=pltpu.HBM)
PARAMS = pltpu.CompilerParams(vmem_limit_bytes=24 << 20)


def column_of(row):
    return jnp.broadcast_to(row, (HD, row.shape[1])).T


def bias_of(query_level, key_level):
    wide = jnp.concatenate([query_level] * (key_level.shape[1] // HD), axis=1)
    return jnp.where(key_level <= wide, 0.0, HIDDEN)


def piece_kernel(where_ref, asked_ref, load_ref, piece_ref):
    tok = load_ref.shape[0] - PAD
    position = where_ref[0]
    odd = lax.rem(position, 2)
    entry = jnp.where(odd == 1, asked_ref[0, 1], asked_ref[0, 2])
    blocks = tok // BLOCK
    first = pl.multiple_of(jnp.clip(entry - position * blocks, 0, blocks - 1) * BLOCK, BLOCK)
    piece_ref[:BLOCK, :] = load_ref[pl.ds(first, BLOCK), :]
    level = load_ref[tok:, pl.ds(first, BLOCK)]
    piece_ref[BLOCK:, :] = jnp.concatenate([level] * (load_ref.shape[1] // BLOCK), axis=1)


def own_kernel(kv_heads, q_ref, load_ref, level_ref, o_ref, lse_ref, bias_ref, vx_ref):
    tok = q_ref.shape[0]
    level = level_ref[...].astype(jnp.float32)
    bias_ref[...] = bias_of(column_of(level), level)
    lane = lax.broadcasted_iota(jnp.int32, (ROWS, HD), 1)
    vx_ref[:, HD:] = jnp.ones((tok, HD), jnp.bfloat16)

    def step(g, carry):
        base = pl.multiple_of(g * (GROUP * HD), GROUP * HD)
        cols = pl.ds(pl.multiple_of(g * HD, HD), HD)
        vx_ref[:, :HD] = load_ref[:tok, pl.ds(pl.multiple_of((g + kv_heads) * HD, HD), HD)]
        for r in range(0, tok, ROWS):
            rows = pl.ds(r, ROWS)
            lse = jnp.zeros((ROWS, HD), jnp.float32)
            for h in range(GROUP):
                head = pl.ds(base + h * HD, HD)
                s = lax.dot_general(q_ref[rows, head], load_ref[:tok, cols], NT, preferred_element_type=jnp.float32)
                s = s * SCALE + bias_ref[rows, :]
                top = jnp.max(s, axis=1, keepdims=True)
                p = jnp.exp2(s - top).astype(jnp.bfloat16)
                o = lax.dot_general(p, vx_ref[...], NN, preferred_element_type=jnp.float32)
                total = o[:, HD:]
                o_ref[rows, head] = o[:, :HD] / total
                lse = jnp.where(lane == h, top + jnp.log2(total), lse)
            lse_ref[g, rows, :] = lse
        return carry

    lax.fori_loop(0, kv_heads, step, 0)


def far_kernel(
    kv_heads, where_ref, members_ref, q_ref, level_ref, o_ref, lse_ref, lo_ref, near_ref, diag_ref, hi_ref,
    out_ref, bias_ref, kx_ref, vx_ref, kl_ref, done_ref, sems,
):
    tok = q_ref.shape[0]
    far = kx_ref.shape[0]
    blocks = tok // BLOCK
    position = where_ref[0]
    odd = lax.rem(position, 2)
    before, after = members_ref[0, 1], members_ref[0, 2]
    near = jnp.where(odd == 1, before, after)
    diag = jnp.where(odd == 1, after, before)
    entries = (
        (lo_ref, members_ref[0, 0], position - 2),
        (near_ref, near, position + 1 - 2 * odd),
        (diag_ref, diag, None),
        (hi_ref, members_ref[0, 3], position + 2),
    )
    firsts = []
    for slot, (ref, entry, owner) in enumerate(entries):
        if owner is None:
            first = 0
            level = ref[BLOCK : BLOCK + 1, :BLOCK]
        else:
            first = pl.multiple_of(jnp.clip(entry - owner * blocks, 0, blocks - 1) * BLOCK, BLOCK)
            level = ref[tok : tok + 1, pl.ds(first, BLOCK)]
        firsts.append(first)
        level = jnp.where(entry >= 0, level.astype(jnp.float32), 1e9)
        kl_ref[0:1, slot * BLOCK : (slot + 1) * BLOCK] = level
    query_level = column_of(level_ref[...].astype(jnp.float32))
    bias_ref[...] = bias_of(query_level, kl_ref[0:1, :])
    vx_ref[:, HD:] = jnp.ones((far, HD), jnp.bfloat16)

    def out_copy(g, r):
        spot = (pl.ds(r, ROWS), pl.ds(pl.multiple_of(g * (GROUP * HD), GROUP * HD), GROUP * HD))
        return pltpu.make_async_copy(done_ref.at[spot], out_ref.at[spot], sems.at[g, r // ROWS])

    def step(g, carry):
        base = pl.multiple_of(g * (GROUP * HD), GROUP * HD)
        cols = pl.ds(pl.multiple_of(g * HD, HD), HD)
        vcols = pl.ds(pl.multiple_of((g + kv_heads) * HD, HD), HD)
        for slot, (ref, _, _) in enumerate(entries):
            picked = pl.ds(firsts[slot], BLOCK)
            kx_ref[slot * BLOCK : (slot + 1) * BLOCK, :] = ref[picked, cols]
            vx_ref[slot * BLOCK : (slot + 1) * BLOCK, :HD] = ref[picked, vcols]
        for r in range(0, tok, ROWS):
            rows = pl.ds(r, ROWS)
            lse = lse_ref[g, rows, :]
            for h in range(GROUP):
                head = pl.ds(base + h * HD, HD)
                own = lse[:, h : h + 1]
                s = lax.dot_general(q_ref[rows, head], kx_ref[...], NT, preferred_element_type=jnp.float32)
                s = s * SCALE + bias_ref[rows, :]
                top = jnp.maximum(jnp.max(s, axis=1, keepdims=True), own)
                p = jnp.exp2(s - top).astype(jnp.bfloat16)
                o = lax.dot_general(p, vx_ref[...], NN, preferred_element_type=jnp.float32)
                share = jnp.exp2(own - top)
                mixed = (o[:, :HD] + share * o_ref[rows, head]) / (o[:, HD:] + share)
                done_ref[rows, head] = mixed.astype(jnp.bfloat16)
            out_copy(g, r).start()
        return carry

    lax.fori_loop(0, kv_heads, step, 0)
    for g in range(kv_heads):
        for r in range(0, tok, ROWS):
            out_copy(g, r).wait()


def pairs_of(size, kind):
    if kind == "near":
        edges = [(i, i + 1) for i in range(0, size - 1, 2)]
        return [p for a, b in edges for p in ((a, b), (b, a))]
    if kind == "diag":
        edges = [(i, i + 1) for i in range(1, size - 1, 2)]
        return [p for a, b in edges for p in ((a, b), (b, a))]
    return [(i, i + kind) for i in range(size) if 0 <= i + kind < size]


def cost_of(tok, keys, heads):
    return pl.CostEstimate(
        flops=4 * tok * keys * heads * HD, transcendentals=tok * keys * heads, bytes_accessed=8 << 20
    )


def local(queries, keys, values, levels, members):
    tok = queries.shape[0]
    kv_heads = keys.shape[1] // HD
    heads = queries.shape[1] // HD
    size = lax.axis_size("seq")
    where = lax.axis_index("seq").astype(jnp.int32)[None]
    level_line = levels[None, :]
    send = lambda array, kind: lax.ppermute(array, "seq", pairs_of(size, kind))
    width = 2 * keys.shape[1]

    asked = send(members, "diag")
    level_rows = jnp.broadcast_to(level_line, (PAD, width)).astype(jnp.bfloat16)
    level_rows, asked = lax.optimization_barrier((level_rows, asked))
    load = jnp.concatenate([jnp.concatenate([keys, values], axis=1), level_rows], axis=0)
    from_hi = send(load, -2)
    from_lo = send(load, 2)
    from_near = send(load, "near")
    piece = pl.pallas_call(
        piece_kernel,
        in_specs=[SMEM, SMEM, VMEM],
        out_specs=VMEM,
        out_shape=jax.ShapeDtypeStruct((BLOCK + PAD, width), jnp.bfloat16),
        compiler_params=PARAMS,
        cost_estimate=pl.CostEstimate(flops=0, transcendentals=0, bytes_accessed=8 << 20),
    )(where, asked, load)
    from_diag = send(piece, "diag")

    part, lse = pl.pallas_call(
        functools.partial(own_kernel, kv_heads),
        in_specs=[VMEM] * 3,
        out_specs=[VMEM] * 2,
        out_shape=[
            jax.ShapeDtypeStruct((tok, heads * HD), jnp.float32),
            jax.ShapeDtypeStruct((kv_heads, tok, HD), jnp.float32),
        ],
        scratch_shapes=[pltpu.VMEM((tok, tok), jnp.float32), pltpu.VMEM((tok, 2 * HD), jnp.bfloat16)],
        compiler_params=PARAMS,
        cost_estimate=cost_of(tok, tok, heads),
    )(queries, load, level_line)

    far = 2 * RADIUS * BLOCK
    return pl.pallas_call(
        functools.partial(far_kernel, kv_heads),
        in_specs=[SMEM] * 2 + [VMEM] * 8,
        out_specs=HBM,
        scratch_shapes=[
            pltpu.VMEM((tok, far), jnp.float32),
            pltpu.VMEM((far, HD), jnp.bfloat16),
            pltpu.VMEM((far, 2 * HD), jnp.bfloat16),
            pltpu.VMEM((8, far), jnp.float32),
            pltpu.VMEM((tok, heads * HD), jnp.bfloat16),
            pltpu.SemaphoreType.DMA((kv_heads, tok // ROWS)),
        ],
        out_shape=jax.ShapeDtypeStruct((tok, heads * HD), jnp.bfloat16),
        compiler_params=PARAMS,
        cost_estimate=cost_of(tok, far, heads),
    )(where, members, queries, level_line, part, lse, from_lo, from_near, from_diag, from_hi)


def solution(mesh):
    placed = (
        P(("grp", "seq"), "head"),
        P(("grp", "seq"), "head"),
        P(("grp", "seq"), "head"),
        P(("grp", "seq")),
        P(("grp", "seq"), None),
    )
    return jax.shard_map(
        local, mesh=mesh, in_specs=placed, out_specs=P(("grp", "seq"), "head"), check_vma=False
    )
```

```python
import functools

import jax
import jax.numpy as jnp
from jax import lax
from jax.experimental import pallas as pl
from jax.experimental.pallas import tpu as pltpu
from jax.sharding import PartitionSpec as P

HD = 128
BLOCK = 128
RADIUS = 2
GROUP = 8
ROWS = 128
PAD = 16
SCALE = HD ** (-0.5) * 1.4426950408889634
HIDDEN = -1e30
NT = (((1,), (1,)), ((), ()))
NN = (((1,), (0,)), ((), ()))
VMEM = pl.BlockSpec(memory_space=pltpu.VMEM)
SMEM = pl.BlockSpec(memory_space=pltpu.SMEM)
HBM = pl.BlockSpec(memory_space=pltpu.HBM)
PARAMS = pltpu.CompilerParams(vmem_limit_bytes=24 << 20)


def column_of(row):
    return jnp.broadcast_to(row, (HD, row.shape[1])).T


def bias_of(query_level, key_level):
    wide = jnp.concatenate([query_level] * (key_level.shape[1] // HD), axis=1)
    return jnp.where(key_level <= wide, 0.0, HIDDEN)


def piece_kernel(where_ref, asked_ref, load_ref, piece_ref):
    tok = load_ref.shape[0] - PAD
    position = where_ref[0]
    odd = lax.rem(position, 2)
    entry = jnp.where(odd == 1, asked_ref[0, 1], asked_ref[0, 2])
    blocks = tok // BLOCK
    first = pl.multiple_of(jnp.clip(entry - position * blocks, 0, blocks - 1) * BLOCK, BLOCK)
    piece_ref[:BLOCK, :] = load_ref[pl.ds(first, BLOCK), :]
    level = load_ref[tok:, pl.ds(first, BLOCK)]
    piece_ref[BLOCK:, :] = jnp.concatenate([level] * (load_ref.shape[1] // BLOCK), axis=1)


def own_kernel(kv_heads, q_hbm, load_ref, o_ref, lse_ref, q_ref, column_ref, bias_ref, vx_ref, sems):
    tok = q_ref.shape[0]

    def q_copy(g):
        spot = (pl.ds(0, tok), pl.ds(pl.multiple_of(g * (GROUP * HD), GROUP * HD), GROUP * HD))
        return pltpu.make_async_copy(q_hbm.at[spot], q_ref.at[spot], sems.at[g])

    for g in range(kv_heads):
        q_copy(g).start()
    level = load_ref[tok : tok + 1, :].astype(jnp.float32)
    column_ref[...] = column_of(level)
    bias_ref[...] = bias_of(column_ref[...], level)
    vx_ref[:, HD:] = jnp.ones((tok, HD), jnp.bfloat16)

    def step(g, carry):
        base = pl.multiple_of(g * (GROUP * HD), GROUP * HD)
        cols = pl.ds(pl.multiple_of(g * HD, HD), HD)
        q_copy(g).wait()
        vx_ref[:, :HD] = load_ref[:tok, pl.ds(pl.multiple_of((g + kv_heads) * HD, HD), HD)]
        for r in range(0, tok, ROWS):
            rows = pl.ds(r, ROWS)
            for h in range(GROUP):
                head = pl.ds(base + h * HD, HD)
                s = lax.dot_general(q_ref[rows, head], load_ref[:tok, cols], NT, preferred_element_type=jnp.float32)
                s = s * SCALE + bias_ref[rows, :]
                top = jnp.max(s, axis=1, keepdims=True)
                p = jnp.exp2(s - top).astype(jnp.bfloat16)
                o = lax.dot_general(p, vx_ref[...], NN, preferred_element_type=jnp.float32)
                total = o[:, HD:]
                o_ref[rows, head] = o[:, :HD] / total
                lse_ref[rows, head] = top + jnp.log2(total)
        return carry

    lax.fori_loop(0, kv_heads, step, 0)


def far_kernel(
    kv_heads, where_ref, members_ref, q_ref, column_ref, o_ref, lse_ref, lo_ref, near_ref, diag_ref, hi_ref,
    out_ref, bias_ref, kx_ref, vx_ref, kl_ref, done_ref, sems,
):
    tok = q_ref.shape[0]
    far = kx_ref.shape[0]
    blocks = tok // BLOCK
    position = where_ref[0]
    odd = lax.rem(position, 2)
    before, after = members_ref[0, 1], members_ref[0, 2]
    flip = lax.rem(lax.div(position, 2), 2) == 1
    lowest, highest = members_ref[0, 0], members_ref[0, 3]
    even, even_owner = jnp.where(flip, lowest, highest), position + jnp.where(flip, -2, 2)
    other, other_owner = jnp.where(flip, highest, lowest), position + jnp.where(flip, 2, -2)
    near = jnp.where(odd == 1, before, after)
    diag = jnp.where(odd == 1, after, before)
    entries = (
        (lo_ref, other, other_owner),
        (near_ref, near, position + 1 - 2 * odd),
        (diag_ref, diag, None),
        (hi_ref, even, even_owner),
    )
    firsts = []
    for slot, (ref, entry, owner) in enumerate(entries):
        if owner is None:
            first = 0
            level = ref[BLOCK : BLOCK + 1, :BLOCK]
        else:
            first = pl.multiple_of(jnp.clip(entry - owner * blocks, 0, blocks - 1) * BLOCK, BLOCK)
            level = ref[tok : tok + 1, pl.ds(first, BLOCK)]
        firsts.append(first)
        level = jnp.where(entry >= 0, level.astype(jnp.float32), 1e9)
        kl_ref[0:1, slot * BLOCK : (slot + 1) * BLOCK] = level
    bias_ref[...] = bias_of(column_ref[...], kl_ref[0:1, :])
    vx_ref[:, HD:] = jnp.ones((far, HD), jnp.bfloat16)

    def out_copy(g, r):
        spot = (pl.ds(r, ROWS), pl.ds(pl.multiple_of(g * (GROUP * HD), GROUP * HD), GROUP * HD))
        return pltpu.make_async_copy(done_ref.at[spot], out_ref.at[spot], sems.at[g, r // ROWS])

    def step(g, carry):
        base = pl.multiple_of(g * (GROUP * HD), GROUP * HD)
        cols = pl.ds(pl.multiple_of(g * HD, HD), HD)
        vcols = pl.ds(pl.multiple_of((g + kv_heads) * HD, HD), HD)
        for slot, (ref, _, _) in enumerate(entries):
            picked = pl.ds(firsts[slot], BLOCK)
            kx_ref[slot * BLOCK : (slot + 1) * BLOCK, :] = ref[picked, cols]
            vx_ref[slot * BLOCK : (slot + 1) * BLOCK, :HD] = ref[picked, vcols]
        for r in range(0, tok, ROWS):
            rows = pl.ds(r, ROWS)
            for h in range(GROUP):
                head = pl.ds(base + h * HD, HD)
                own = lse_ref[rows, head]
                s = lax.dot_general(q_ref[rows, head], kx_ref[...], NT, preferred_element_type=jnp.float32)
                s = s * SCALE + bias_ref[rows, :]
                tops = [s[:, i : i + HD] for i in range(0, far, HD)]
                top = jnp.max(functools.reduce(jnp.maximum, tops, own), axis=1, keepdims=True)
                p = jnp.exp2(s - top).astype(jnp.bfloat16)
                o = lax.dot_general(p, vx_ref[...], NN, preferred_element_type=jnp.float32)
                share = jnp.exp2(own - top)
                mixed = (o[:, :HD] + share * o_ref[rows, head]) / (o[:, HD:] + share)
                done_ref[rows, head] = mixed.astype(jnp.bfloat16)
            out_copy(g, r).start()
        return carry

    lax.fori_loop(0, kv_heads, step, 0)
    for g in range(kv_heads):
        for r in range(0, tok, ROWS):
            out_copy(g, r).wait()


def pairs_of(size, kind):
    if kind == "near":
        edges = [(i, i + 1) for i in range(0, size - 1, 2)]
        return [p for a, b in edges for p in ((a, b), (b, a))]
    if kind == "diag":
        edges = [(i, i + 1) for i in range(1, size - 1, 2)]
        return [p for a, b in edges for p in ((a, b), (b, a))]
    edges = [(i, i + 2) for i in range(size - 2) if (i // 2) % 2 == (kind == "odd")]
    return [p for a, b in edges for p in ((a, b), (b, a))]


def cost_of(tok, keys, heads):
    return pl.CostEstimate(
        flops=4 * tok * keys * heads * HD, transcendentals=tok * keys * heads, bytes_accessed=8 << 20
    )


def local(queries, keys, values, levels, members):
    tok = queries.shape[0]
    kv_heads = keys.shape[1] // HD
    heads = queries.shape[1] // HD
    size = lax.axis_size("seq")
    where = lax.axis_index("seq").astype(jnp.int32)[None]
    level_line = levels[None, :]
    send = lambda array, kind: lax.ppermute(array, "seq", pairs_of(size, kind))
    width = 2 * keys.shape[1]

    asked = send(members, "diag")
    level_rows = jnp.broadcast_to(level_line, (PAD, width)).astype(jnp.bfloat16)
    load = jnp.concatenate([jnp.concatenate([keys, values], axis=1), level_rows], axis=0)
    load, asked = lax.optimization_barrier((load, asked))
    from_hi = send(load, "even")
    from_lo = send(load, "odd")
    from_near = send(load, "near")
    piece = pl.pallas_call(
        piece_kernel,
        in_specs=[SMEM, SMEM, VMEM],
        out_specs=VMEM,
        out_shape=jax.ShapeDtypeStruct((BLOCK + PAD, width), jnp.bfloat16),
        compiler_params=PARAMS,
        cost_estimate=pl.CostEstimate(flops=0, transcendentals=0, bytes_accessed=8 << 20),
    )(where, asked, load)
    from_diag = send(piece, "diag")

    part, lse, rows_in, column = pl.pallas_call(
        functools.partial(own_kernel, kv_heads),
        in_specs=[HBM, VMEM],
        out_specs=[VMEM] * 4,
        out_shape=[
            jax.ShapeDtypeStruct((tok, heads * HD), jnp.float32),
            jax.ShapeDtypeStruct((tok, heads * HD), jnp.float32),
            jax.ShapeDtypeStruct((tok, heads * HD), jnp.bfloat16),
            jax.ShapeDtypeStruct((tok, HD), jnp.float32),
        ],
        scratch_shapes=[
            pltpu.VMEM((tok, tok), jnp.float32),
            pltpu.VMEM((tok, 2 * HD), jnp.bfloat16),
            pltpu.SemaphoreType.DMA((kv_heads,)),
        ],
        compiler_params=PARAMS,
        cost_estimate=cost_of(tok, tok, heads),
    )(pltpu.with_memory_space_constraint(queries, pltpu.HBM), load)

    far = 2 * RADIUS * BLOCK
    return pl.pallas_call(
        functools.partial(far_kernel, kv_heads),
        in_specs=[SMEM] * 2 + [VMEM] * 8,
        out_specs=HBM,
        scratch_shapes=[
            pltpu.VMEM((tok, far), jnp.float32),
            pltpu.VMEM((far, HD), jnp.bfloat16),
            pltpu.VMEM((far, 2 * HD), jnp.bfloat16),
            pltpu.VMEM((8, far), jnp.float32),
            pltpu.VMEM((tok, heads * HD), jnp.bfloat16),
            pltpu.SemaphoreType.DMA((kv_heads, tok // ROWS)),
        ],
        out_shape=jax.ShapeDtypeStruct((tok, heads * HD), jnp.bfloat16),
        compiler_params=PARAMS,
        cost_estimate=cost_of(tok, far, heads),
    )(where, members, rows_in, column, part, lse, from_lo, from_near, from_diag, from_hi)


def solution(mesh):
    placed = (
        P(("grp", "seq"), "head"),
        P(("grp", "seq"), "head"),
        P(("grp", "seq"), "head"),
        P(("grp", "seq")),
        P(("grp", "seq"), None),
    )
    return jax.shard_map(
        local, mesh=mesh, in_specs=placed, out_specs=P(("grp", "seq"), "head"), check_vma=False
    )
```

```python
import functools

import jax
import jax.numpy as jnp
from jax import lax
from jax.experimental import pallas as pl
from jax.experimental.pallas import tpu as pltpu
from jax.sharding import PartitionSpec as P

HD = 128
BLOCK = 128
GROUP = 8
ROWS = 256
PAD = 16
EARLY = 2
PICKED = ("even", "odd", "near", "diag")
SOURCES = ("even", "near", "odd", "diag")
SCALE = HD ** (-0.5) * 1.4426950408889634
HIDDEN = -1e30
NT = (((1,), (1,)), ((), ()))
NN = (((1,), (0,)), ((), ()))
VMEM = pl.BlockSpec(memory_space=pltpu.VMEM)
SMEM = pl.BlockSpec(memory_space=pltpu.SMEM)
HBM = pl.BlockSpec(memory_space=pltpu.HBM)
PARAMS = pltpu.CompilerParams(vmem_limit_bytes=24 << 20)


def column_of(row):
    return jnp.broadcast_to(row, (HD, row.shape[1])).T


def bias_of(query_level, key_level):
    wide = jnp.concatenate([query_level] * (key_level.shape[1] // HD), axis=1)
    return jnp.where(key_level <= wide, 0.0, HIDDEN)


def attend_own(kv_heads, chosen, q_ref, load_ref, acc_ref, top_ref, bias_ref, vx_ref):
    tok = q_ref.shape[0]
    vx_ref[:, HD:] = jnp.ones((tok, HD), jnp.bfloat16)
    for g in range(kv_heads):
        mine = [h for h in chosen if h // GROUP == g]
        if not mine:
            continue
        keys = load_ref[:tok, g * HD : (g + 1) * HD]
        vx_ref[:, :HD] = load_ref[:tok, (g + kv_heads) * HD : (g + kv_heads + 1) * HD]
        for r in range(0, tok, ROWS):
            rows = pl.ds(r, ROWS)
            for h in mine:
                spot = pl.ds((h - chosen[0]) * HD, HD)
                s = lax.dot_general(
                    q_ref[rows, h * HD : (h + 1) * HD], keys, NT, preferred_element_type=jnp.float32
                )
                s = s * SCALE + bias_ref[rows, :]
                top = jnp.max(s, axis=1, keepdims=True)
                p = jnp.exp2(s - top).astype(jnp.bfloat16)
                o = lax.dot_general(p, vx_ref[...], NN, preferred_element_type=jnp.float32)
                total = o[:, HD:]
                acc_ref[rows, spot] = o[:, :HD] / total
                top_ref[rows, spot] = top + jnp.log2(total)


def pack_kernel(
    kv_heads, k_hbm, v_hbm, q_hbm, level_hbm, load_ref, q_ref, column_ref, acc_ref, top_ref,
    level_ref, bias_ref, vx_ref, sems,
):
    tok, width = k_hbm.shape
    early = EARLY * HD
    rest = q_hbm.shape[1] - early
    copies = [
        pltpu.make_async_copy(level_hbm, level_ref, sems.at[0]),
        pltpu.make_async_copy(k_hbm, load_ref.at[pl.ds(0, tok), pl.ds(0, width)], sems.at[1]),
        pltpu.make_async_copy(v_hbm, load_ref.at[pl.ds(0, tok), pl.ds(width, width)], sems.at[2]),
        pltpu.make_async_copy(q_hbm.at[:, pl.ds(0, early)], q_ref.at[:, pl.ds(0, early)], sems.at[3]),
        pltpu.make_async_copy(q_hbm.at[:, pl.ds(early, rest)], q_ref.at[:, pl.ds(early, rest)], sems.at[4]),
    ]
    for copy in copies:
        copy.start()
    copies[0].wait()
    level = level_ref[...].astype(jnp.float32)
    load_ref[tok:, :] = jnp.broadcast_to(level, (PAD, tok)).astype(jnp.bfloat16)
    column_ref[...] = column_of(level)
    bias_ref[...] = bias_of(column_ref[...], level)
    for copy in copies[1:4]:
        copy.wait()
    attend_own(kv_heads, range(EARLY), q_ref, load_ref, acc_ref, top_ref, bias_ref, vx_ref)
    copies[4].wait()


def piece_kernel(sources, where_ref, *refs):
    count = len(sources)
    load_ref = refs[count]
    tok = load_ref.shape[0] - PAD
    position = where_ref[0]
    blocks = tok // BLOCK
    for source, asked_ref, piece_ref in zip(sources, refs[:count], refs[count + 1 :]):
        entry = asked_ref[0, partner_of(source, position)[2]]
        first = pl.multiple_of(jnp.clip(entry - position * blocks, 0, blocks - 1) * BLOCK, BLOCK)
        piece_ref[:BLOCK, :] = load_ref[pl.ds(first, BLOCK), :]
        level = load_ref[tok:, pl.ds(first, BLOCK)]
        piece_ref[BLOCK:, :] = jnp.concatenate([level] * (load_ref.shape[1] // BLOCK), axis=1)


def own_kernel(kv_heads, q_ref, load_ref, column_ref, acc_ref, top_ref, bias_ref, vx_ref):
    tok = q_ref.shape[0]
    bias_ref[...] = bias_of(column_ref[...], load_ref[tok : tok + 1, :].astype(jnp.float32))
    late = range(EARLY, q_ref.shape[1] // HD)
    attend_own(kv_heads, late, q_ref, load_ref, acc_ref, top_ref, bias_ref, vx_ref)


def partner_of(source, position):
    if source in ("even", "odd"):
        above = (lax.rem(lax.div(position, 2), 2) == 0) == (source == "even")
        return jnp.where(above, 2, -2), jnp.where(above, 3, 0), jnp.where(above, 0, 3)
    above = (lax.rem(position, 2) == 0) == (source == "near")
    return jnp.where(above, 1, -1), jnp.where(above, 2, 1), jnp.where(above, 1, 2)


def pick_of(source, where_ref, members_ref, ref):
    position = where_ref[0]
    offset, column, _ = partner_of(source, position)
    entry = members_ref[0, column]
    if ref.shape[0] == BLOCK + PAD:
        return entry, 0, ref[BLOCK : BLOCK + 1, :BLOCK]
    tok = ref.shape[0] - PAD
    blocks = tok // BLOCK
    first = pl.multiple_of(jnp.clip(entry - (position + offset) * blocks, 0, blocks - 1) * BLOCK, BLOCK)
    return entry, first, ref[tok : tok + 1, pl.ds(first, BLOCK)]


def far_kernel(kv_heads, where_ref, members_ref, q_ref, column_ref, acc0_ref, top0_ref, acc1_ref, top1_ref, *refs):
    source_refs = refs[: len(SOURCES)]
    out_ref, bias_ref, kx_ref, vx_ref, kl_ref, done_ref, sems = refs[len(SOURCES) :]
    tok = q_ref.shape[0]
    far = len(SOURCES) * BLOCK
    firsts = []
    for slot, (source, ref) in enumerate(zip(SOURCES, source_refs)):
        entry, first, level = pick_of(source, where_ref, members_ref, ref)
        firsts.append(first)
        kl_ref[0:1, slot * BLOCK : (slot + 1) * BLOCK] = jnp.where(entry >= 0, level.astype(jnp.float32), 1e9)
    bias_ref[...] = bias_of(column_ref[...], kl_ref[0:1, :])
    vx_ref[:, HD:] = jnp.ones((far, HD), jnp.bfloat16)

    def out_copy(g, r):
        spot = (pl.ds(r, ROWS), pl.ds(g * GROUP * HD, GROUP * HD))
        return pltpu.make_async_copy(done_ref.at[spot], out_ref.at[spot], sems.at[g, r // ROWS])

    for g in range(kv_heads):
        cols = pl.ds(g * HD, HD)
        vcols = pl.ds((g + kv_heads) * HD, HD)
        for slot, ref in enumerate(source_refs):
            picked = pl.ds(firsts[slot], BLOCK)
            kx_ref[slot * BLOCK : (slot + 1) * BLOCK, :] = ref[picked, cols]
            vx_ref[slot * BLOCK : (slot + 1) * BLOCK, :HD] = ref[picked, vcols]
        for r in range(0, tok, ROWS):
            rows = pl.ds(r, ROWS)
            for h in range(g * GROUP, (g + 1) * GROUP):
                head = pl.ds(h * HD, HD)
                if h < EARLY:
                    acc_ref, top_ref, spot = acc0_ref, top0_ref, pl.ds(h * HD, HD)
                else:
                    acc_ref, top_ref, spot = acc1_ref, top1_ref, pl.ds((h - EARLY) * HD, HD)
                old = top_ref[rows, spot]
                s = lax.dot_general(q_ref[rows, head], kx_ref[...], NT, preferred_element_type=jnp.float32)
                s = s * SCALE + bias_ref[rows, :]
                tops = [s[:, i : i + HD] for i in range(0, far, HD)]
                top = jnp.max(functools.reduce(jnp.maximum, tops, old), axis=1, keepdims=True)
                p = jnp.exp2(s - top).astype(jnp.bfloat16)
                o = lax.dot_general(p, vx_ref[...], NN, preferred_element_type=jnp.float32)
                share = jnp.exp2(old - top)
                mixed = (o[:, :HD] + share * acc_ref[rows, spot]) / (o[:, HD:] + share)
                done_ref[rows, head] = mixed.astype(jnp.bfloat16)
            out_copy(g, r).start()
    for g in range(kv_heads):
        for r in range(0, tok, ROWS):
            out_copy(g, r).wait()


def pairs_of(size, kind):
    if kind == "near":
        edges = [(i, i + 1) for i in range(0, size - 1, 2)]
        return [p for a, b in edges for p in ((a, b), (b, a))]
    if kind == "diag":
        edges = [(i, i + 1) for i in range(1, size - 1, 2)]
        return [p for a, b in edges for p in ((a, b), (b, a))]
    edges = [(i, i + 2) for i in range(size - 2) if (i // 2) % 2 == (kind == "odd")]
    return [p for a, b in edges for p in ((a, b), (b, a))]


def cost_of(tok, keys, heads):
    return pl.CostEstimate(
        flops=4 * tok * keys * heads * HD, transcendentals=tok * keys * heads, bytes_accessed=8 << 20
    )


def local(queries, keys, values, levels, members):
    tok = queries.shape[0]
    kv_heads = keys.shape[1] // HD
    heads = queries.shape[1] // HD
    size = lax.axis_size("seq")
    where = lax.axis_index("seq").astype(jnp.int32)[None]
    level_line = levels[None, :]
    send = lambda array, kind: lax.ppermute(array, "seq", pairs_of(size, kind))
    width = 2 * keys.shape[1]

    asked = {kind: send(members, kind) for kind in PICKED}
    wide = lambda count: jax.ShapeDtypeStruct((tok, count * HD), jnp.float32)
    rows_type = jax.ShapeDtypeStruct((tok, heads * HD), jnp.bfloat16)
    stay = lambda array: pltpu.with_memory_space_constraint(array, pltpu.HBM)
    own_scratch = [pltpu.VMEM((tok, tok), jnp.float32), pltpu.VMEM((tok, 2 * HD), jnp.bfloat16)]
    load, rows_in, column, acc0, top0 = pl.pallas_call(
        functools.partial(pack_kernel, kv_heads),
        in_specs=[HBM] * 4,
        out_specs=[VMEM] * 5,
        out_shape=[
            jax.ShapeDtypeStruct((tok + PAD, width), jnp.bfloat16),
            rows_type,
            wide(1),
            wide(EARLY),
            wide(EARLY),
        ],
        scratch_shapes=[pltpu.VMEM((1, tok), jnp.int32)] + own_scratch + [pltpu.SemaphoreType.DMA((5,))],
        compiler_params=PARAMS,
        cost_estimate=cost_of(tok, tok, EARLY),
    )(stay(keys), stay(values), stay(queries), stay(level_line))
    load, asked = lax.optimization_barrier((load, asked))
    arrived = {kind: send(load, kind) for kind in SOURCES if kind not in PICKED}
    pieces = pl.pallas_call(
        functools.partial(piece_kernel, PICKED),
        in_specs=[SMEM] * (1 + len(PICKED)) + [VMEM],
        out_specs=[VMEM] * len(PICKED),
        out_shape=[jax.ShapeDtypeStruct((BLOCK + PAD, width), jnp.bfloat16)] * len(PICKED),
        compiler_params=PARAMS,
        cost_estimate=pl.CostEstimate(flops=0, transcendentals=0, bytes_accessed=8 << 20),
    )(where, *[asked[kind] for kind in PICKED], load)
    arrived |= {kind: send(piece, kind) for kind, piece in zip(PICKED, pieces)}

    acc1, top1 = pl.pallas_call(
        functools.partial(own_kernel, kv_heads),
        in_specs=[VMEM] * 3,
        out_specs=[VMEM] * 2,
        out_shape=[wide(heads - EARLY)] * 2,
        scratch_shapes=own_scratch,
        compiler_params=PARAMS,
        cost_estimate=cost_of(tok, tok, heads - EARLY),
    )(rows_in, load, column)

    far = len(SOURCES) * BLOCK
    return pl.pallas_call(
        functools.partial(far_kernel, kv_heads),
        in_specs=[SMEM] * 2 + [VMEM] * (6 + len(SOURCES)),
        out_specs=HBM,
        out_shape=rows_type,
        scratch_shapes=[
            pltpu.VMEM((tok, far), jnp.float32),
            pltpu.VMEM((far, HD), jnp.bfloat16),
            pltpu.VMEM((far, 2 * HD), jnp.bfloat16),
            pltpu.VMEM((8, far), jnp.float32),
            pltpu.VMEM((tok, heads * HD), jnp.bfloat16),
            pltpu.SemaphoreType.DMA((kv_heads, tok // ROWS)),
        ],
        compiler_params=PARAMS,
        cost_estimate=cost_of(tok, far, heads),
    )(where, members, rows_in, column, acc0, top0, acc1, top1, *[arrived[kind] for kind in SOURCES])


def solution(mesh):
    placed = (
        P(("grp", "seq"), "head"),
        P(("grp", "seq"), "head"),
        P(("grp", "seq"), "head"),
        P(("grp", "seq")),
        P(("grp", "seq"), None),
    )
    return jax.shard_map(
        local, mesh=mesh, in_specs=placed, out_specs=P(("grp", "seq"), "head"), check_vma=False
    )
```

```python
import functools

import jax
import jax.numpy as jnp
from jax import lax
from jax.experimental import pallas as pl
from jax.experimental.pallas import tpu as pltpu
from jax.sharding import PartitionSpec as P

HD = 128
BLOCK = 128
GROUP = 8
ROWS = 256
PAD = 16
EARLY = 2
SPAN = 4
PICKED = ("even", "odd", "near", "diag")
SOURCES = ("near", "even", "odd", "diag")
SCALE = HD ** (-0.5) * 1.4426950408889634
HIDDEN = -1e30
NT = (((1,), (1,)), ((), ()))
NN = (((1,), (0,)), ((), ()))
VMEM = pl.BlockSpec(memory_space=pltpu.VMEM)
SMEM = pl.BlockSpec(memory_space=pltpu.SMEM)
HBM = pl.BlockSpec(memory_space=pltpu.HBM)
PARAMS = pltpu.CompilerParams(vmem_limit_bytes=24 << 20)


def column_of(row):
    return jnp.broadcast_to(row, (HD, row.shape[1])).T


def bias_of(query_level, key_level):
    wide = jnp.concatenate([query_level] * (key_level.shape[1] // HD), axis=1)
    return jnp.where(key_level <= wide, 0.0, HIDDEN)


def attend_own(kv_heads, chosen, q_ref, load_ref, acc_ref, top_ref, bias_ref, vx_ref):
    tok = q_ref.shape[0]
    vx_ref[:, HD:] = jnp.ones((tok, HD), jnp.bfloat16)
    for g in range(kv_heads):
        mine = [h for h in chosen if h // GROUP == g]
        if not mine:
            continue
        keys = load_ref[:tok, g * HD : (g + 1) * HD]
        vx_ref[:, :HD] = load_ref[:tok, (g + kv_heads) * HD : (g + kv_heads + 1) * HD]
        for r in range(0, tok, ROWS):
            rows = pl.ds(r, ROWS)
            for h in mine:
                spot = pl.ds((h - chosen[0]) * HD, HD)
                s = lax.dot_general(
                    q_ref[rows, h * HD : (h + 1) * HD], keys, NT, preferred_element_type=jnp.float32
                )
                s = s * SCALE + bias_ref[rows, :]
                top = jnp.max(s, axis=1, keepdims=True)
                p = jnp.exp2(s - top).astype(jnp.bfloat16)
                o = lax.dot_general(p, vx_ref[...], NN, preferred_element_type=jnp.float32)
                total = o[:, HD:]
                acc_ref[rows, spot] = o[:, :HD] / total
                top_ref[rows, spot] = top + jnp.log2(total)


def pack_kernel(
    kv_heads, k_hbm, v_hbm, q_hbm, level_hbm, load_ref, q_ref, column_ref, acc_ref, top_ref,
    level_ref, bias_ref, vx_ref, sems,
):
    tok, width = k_hbm.shape
    early = EARLY * HD
    rest = q_hbm.shape[1] - early
    copies = [
        pltpu.make_async_copy(level_hbm, level_ref, sems.at[0]),
        pltpu.make_async_copy(k_hbm, load_ref.at[pl.ds(0, tok), pl.ds(0, width)], sems.at[1]),
        pltpu.make_async_copy(v_hbm, load_ref.at[pl.ds(0, tok), pl.ds(width, width)], sems.at[2]),
        pltpu.make_async_copy(q_hbm.at[:, pl.ds(0, early)], q_ref.at[:, pl.ds(0, early)], sems.at[3]),
        pltpu.make_async_copy(q_hbm.at[:, pl.ds(early, rest)], q_ref.at[:, pl.ds(early, rest)], sems.at[4]),
    ]
    for copy in copies:
        copy.start()
    copies[0].wait()
    level = level_ref[...].astype(jnp.float32)
    load_ref[tok:, :] = jnp.broadcast_to(level, (PAD, tok)).astype(jnp.bfloat16)
    column_ref[...] = column_of(level)
    bias_ref[...] = bias_of(column_ref[...], level)
    for copy in copies[1:4]:
        copy.wait()
    attend_own(kv_heads, range(EARLY), q_ref, load_ref, acc_ref, top_ref, bias_ref, vx_ref)
    copies[4].wait()


def piece_kernel(sources, where_ref, *refs):
    count = len(sources)
    load_ref = refs[count]
    tok = load_ref.shape[0] - PAD
    position = where_ref[0]
    blocks = tok // BLOCK
    for source, asked_ref, piece_ref in zip(sources, refs[:count], refs[count + 1 :]):
        entry = asked_ref[0, partner_of(source, position)[2]]
        first = pl.multiple_of(jnp.clip(entry - position * blocks, 0, blocks - 1) * BLOCK, BLOCK)
        piece_ref[:BLOCK, :] = load_ref[pl.ds(first, BLOCK), :]
        level = load_ref[tok:, pl.ds(first, BLOCK)]
        piece_ref[BLOCK:, :] = jnp.concatenate([level] * (load_ref.shape[1] // BLOCK), axis=1)


def own_kernel(kv_heads, q_ref, load_ref, column_ref, acc_ref, top_ref, bias_ref, vx_ref):
    tok = q_ref.shape[0]
    bias_ref[...] = bias_of(column_ref[...], load_ref[tok : tok + 1, :].astype(jnp.float32))
    late = range(EARLY, q_ref.shape[1] // HD)
    attend_own(kv_heads, late, q_ref, load_ref, acc_ref, top_ref, bias_ref, vx_ref)


def partner_of(source, position):
    if source in ("even", "odd"):
        above = (lax.rem(lax.div(position, 2), 2) == 0) == (source == "even")
        return jnp.where(above, 2, -2), jnp.where(above, 3, 0), jnp.where(above, 0, 3)
    above = (lax.rem(position, 2) == 0) == (source == "near")
    return jnp.where(above, 1, -1), jnp.where(above, 2, 1), jnp.where(above, 1, 2)


def pick_of(source, where_ref, members_ref, ref):
    position = where_ref[0]
    offset, column, _ = partner_of(source, position)
    entry = members_ref[0, column]
    if ref.shape[0] == BLOCK + PAD:
        return entry, 0, ref[BLOCK : BLOCK + 1, :BLOCK]
    tok = ref.shape[0] - PAD
    blocks = tok // BLOCK
    first = pl.multiple_of(jnp.clip(entry - (position + offset) * blocks, 0, blocks - 1) * BLOCK, BLOCK)
    return entry, first, ref[tok : tok + 1, pl.ds(first, BLOCK)]


def far_kernel(kv_heads, where_ref, members_ref, q_ref, column_ref, acc0_ref, top0_ref, acc1_ref, top1_ref, *refs):
    source_refs = refs[: len(SOURCES)]
    out_ref, bias_ref, kx_ref, vx_ref, kl_ref, done_ref, sems = refs[len(SOURCES) :]
    tok = q_ref.shape[0]
    far = len(SOURCES) * BLOCK
    firsts = []
    for slot, (source, ref) in enumerate(zip(SOURCES, source_refs)):
        entry, first, level = pick_of(source, where_ref, members_ref, ref)
        firsts.append(first)
        kl_ref[0:1, slot * BLOCK : (slot + 1) * BLOCK] = jnp.where(entry >= 0, level.astype(jnp.float32), 1e9)
    bias_ref[...] = bias_of(column_ref[...], kl_ref[0:1, :])
    vx_ref[:, HD:] = jnp.ones((far, HD), jnp.bfloat16)

    def out_copy(h, r):
        spot = (pl.ds(r, ROWS), pl.ds(h * HD, SPAN * HD))
        return pltpu.make_async_copy(done_ref.at[spot], out_ref.at[spot], sems.at[h // SPAN, r // ROWS])

    for g in range(kv_heads):
        cols = pl.ds(g * HD, HD)
        vcols = pl.ds((g + kv_heads) * HD, HD)
        for slot, ref in enumerate(source_refs):
            picked = pl.ds(firsts[slot], BLOCK)
            kx_ref[slot * BLOCK : (slot + 1) * BLOCK, :] = ref[picked, cols]
            vx_ref[slot * BLOCK : (slot + 1) * BLOCK, :HD] = ref[picked, vcols]
        for r in range(0, tok, ROWS):
            rows = pl.ds(r, ROWS)
            for h in range(g * GROUP, (g + 1) * GROUP):
                head = pl.ds(h * HD, HD)
                if h < EARLY:
                    acc_ref, top_ref, spot = acc0_ref, top0_ref, pl.ds(h * HD, HD)
                else:
                    acc_ref, top_ref, spot = acc1_ref, top1_ref, pl.ds((h - EARLY) * HD, HD)
                old = top_ref[rows, spot]
                s = lax.dot_general(q_ref[rows, head], kx_ref[...], NT, preferred_element_type=jnp.float32)
                s = s * SCALE + bias_ref[rows, :]
                tops = [s[:, i : i + HD] for i in range(0, far, HD)]
                top = jnp.max(functools.reduce(jnp.maximum, tops, old), axis=1, keepdims=True)
                p = jnp.exp2(s - top).astype(jnp.bfloat16)
                o = lax.dot_general(p, vx_ref[...], NN, preferred_element_type=jnp.float32)
                share = jnp.exp2(old - top)
                mixed = (o[:, :HD] + share * acc_ref[rows, spot]) / (o[:, HD:] + share)
                done_ref[rows, head] = mixed.astype(jnp.bfloat16)
                if h % SPAN == SPAN - 1:
                    out_copy(h - SPAN + 1, r).start()
    for h in range(0, kv_heads * GROUP, SPAN):
        for r in range(0, tok, ROWS):
            out_copy(h, r).wait()


def pairs_of(size, kind):
    if kind == "near":
        edges = [(i, i + 1) for i in range(0, size - 1, 2)]
        return [p for a, b in edges for p in ((a, b), (b, a))]
    if kind == "diag":
        edges = [(i, i + 1) for i in range(1, size - 1, 2)]
        return [p for a, b in edges for p in ((a, b), (b, a))]
    edges = [(i, i + 2) for i in range(size - 2) if (i // 2) % 2 == (kind == "odd")]
    return [p for a, b in edges for p in ((a, b), (b, a))]


def cost_of(tok, keys, heads):
    return pl.CostEstimate(
        flops=4 * tok * keys * heads * HD, transcendentals=tok * keys * heads, bytes_accessed=8 << 20
    )


def local(queries, keys, values, levels, members):
    tok = queries.shape[0]
    kv_heads = keys.shape[1] // HD
    heads = queries.shape[1] // HD
    size = lax.axis_size("seq")
    where = lax.axis_index("seq").astype(jnp.int32)[None]
    level_line = levels[None, :]
    send = lambda array, kind: lax.ppermute(array, "seq", pairs_of(size, kind))
    width = 2 * keys.shape[1]

    asked = {kind: send(members, kind) for kind in PICKED}
    wide = lambda count: jax.ShapeDtypeStruct((tok, count * HD), jnp.float32)
    rows_type = jax.ShapeDtypeStruct((tok, heads * HD), jnp.bfloat16)
    stay = lambda array: pltpu.with_memory_space_constraint(array, pltpu.HBM)
    own_scratch = [pltpu.VMEM((tok, tok), jnp.float32), pltpu.VMEM((tok, 2 * HD), jnp.bfloat16)]
    load, rows_in, column, acc0, top0 = pl.pallas_call(
        functools.partial(pack_kernel, kv_heads),
        in_specs=[HBM] * 4,
        out_specs=[VMEM] * 5,
        out_shape=[
            jax.ShapeDtypeStruct((tok + PAD, width), jnp.bfloat16),
            rows_type,
            wide(1),
            wide(EARLY),
            wide(EARLY),
        ],
        scratch_shapes=[pltpu.VMEM((1, tok), jnp.int32)] + own_scratch + [pltpu.SemaphoreType.DMA((5,))],
        compiler_params=PARAMS,
        cost_estimate=cost_of(tok, tok, EARLY),
    )(stay(keys), stay(values), stay(queries), stay(level_line))
    load, asked = lax.optimization_barrier((load, asked))
    arrived = {kind: send(load, kind) for kind in SOURCES if kind not in PICKED}
    pieces = pl.pallas_call(
        functools.partial(piece_kernel, PICKED),
        in_specs=[SMEM] * (1 + len(PICKED)) + [VMEM],
        out_specs=[VMEM] * len(PICKED),
        out_shape=[jax.ShapeDtypeStruct((BLOCK + PAD, width), jnp.bfloat16)] * len(PICKED),
        compiler_params=PARAMS,
        cost_estimate=pl.CostEstimate(flops=0, transcendentals=0, bytes_accessed=8 << 20),
    )(where, *[asked[kind] for kind in PICKED], load)
    arrived |= {kind: send(piece, kind) for kind, piece in zip(PICKED, pieces)}

    acc1, top1 = pl.pallas_call(
        functools.partial(own_kernel, kv_heads),
        in_specs=[VMEM] * 3,
        out_specs=[VMEM] * 2,
        out_shape=[wide(heads - EARLY)] * 2,
        scratch_shapes=own_scratch,
        compiler_params=PARAMS,
        cost_estimate=cost_of(tok, tok, heads - EARLY),
    )(rows_in, load, column)

    far = len(SOURCES) * BLOCK
    return pl.pallas_call(
        functools.partial(far_kernel, kv_heads),
        in_specs=[SMEM] * 2 + [VMEM] * (6 + len(SOURCES)),
        out_specs=HBM,
        out_shape=rows_type,
        scratch_shapes=[
            pltpu.VMEM((tok, far), jnp.float32),
            pltpu.VMEM((far, HD), jnp.bfloat16),
            pltpu.VMEM((far, 2 * HD), jnp.bfloat16),
            pltpu.VMEM((8, far), jnp.float32),
            pltpu.VMEM((tok, heads * HD), jnp.bfloat16),
            pltpu.SemaphoreType.DMA((heads // SPAN, tok // ROWS)),
        ],
        compiler_params=PARAMS,
        cost_estimate=cost_of(tok, far, heads),
    )(where, members, rows_in, column, acc0, top0, acc1, top1, *[arrived[kind] for kind in SOURCES])


def solution(mesh):
    placed = (
        P(("grp", "seq"), "head"),
        P(("grp", "seq"), "head"),
        P(("grp", "seq"), "head"),
        P(("grp", "seq")),
        P(("grp", "seq"), None),
    )
    return jax.shard_map(
        local, mesh=mesh, in_specs=placed, out_specs=P(("grp", "seq"), "head"), check_vma=False
    )
```
